256 devices in a mesh: gx: 8 (over x, core), gy: 4 (over y), gz: 8 (over z).
Axes of the slice: x: 4, y: 4, z: 8, core: 2. Of those that a mesh axis runs over, the one named last changes fastest.
Arguments:
- blocks: bfloat16 [4096, 128, 1024], P(('gx', 'gy', 'gz')), may hold values from -0.375 to 0.375
- counts: int32 [4096], P(('gx', 'gy', 'gz')), may hold values from 1 to 128
- owner: int32 [4096, 1], P(('gx', 'gy', 'gz')), may hold values from 0 to 31; in each aligned block of 16 rows (0 to 15, 16 to 31, ...) no two rows name the same one
- kdiag: float32 [256, 1024], P(('gx', 'gy', 'gz')), may hold values from 0.5 to 4
- rhs: float32 [256, 1024], P(('gx', 'gy', 'gz')), may hold values from -40 to 40
- modes: float32 [256, 6, 1024], P(('gx', 'gy', 'gz')), may hold values from -6 to 6
Outputs:
- schur: bfloat16 [256, 1024, 1024], P(('gx', 'gy', 'gz'))
- solution: float32 [256, 1024], P(('gx', 'gy', 'gz'))
- residual: float32 [256, 1024], P(('gx', 'gy', 'gz'))
The draws below stay inside these ranges and needn't reach their ends.
Inputs may be any that keep to these rules, and one draw needn't show every extreme that they name: `owner`: the 16 blocks of one device go to different owners.
All inputs are finite; a program needn't handle non-finite values.
Results may differ from the reference program's by a relative error of at most 0.001.
Values may be sent and summed in bfloat16 or wider, within the bound.
No kernel may reach another device: no remote copies, remote signals or barrier semaphores. Data moves between devices by JAX's collectives and lax.ppermute only.
A program may use at most 64 MiB of HBM per device.

```python
import math
import jax
import jax.numpy as jnp
import numpy as np
from jax import lax

NB = 1024
ROWS = 128
BLK_DEV = 16
NC = 6
ITERS = 2
SUBDOMAINS = 256
BLOCKS = 4096
N_GX = 8
N_GY = 4
N_GZ = 8


def draw_rhs(key, part):
    index = jnp.arange(SUBDOMAINS, dtype=jnp.float32)[:, None]
    scale = 4.0 * (1.0 + 2.0 * index / max(SUBDOMAINS - 1, 1))
    values = jax.random.normal(jax.random.fold_in(key, 11), (SUBDOMAINS, NB), jnp.float32) * scale
    return jnp.clip(values, -40.0, 40.0)


def touch_ends(values, own_key, least, high):
    shape = values.shape
    place = [jax.random.randint(jax.random.fold_in(own_key, axis), (), 0, shape[axis]) for axis in range(len(shape))]
    values = values.at[tuple(place)].set(least)
    longest = shape.index(max(shape))
    place[longest] = (place[longest] + 1) % shape[longest]
    return values.at[tuple(place)].set(high)


def levels(rng, dims, cuts, low, top_value):
    def one(axis_at, parts):
        heights = jax.random.uniform(jax.random.fold_in(jax.random.fold_in(rng, 6), axis_at), (parts,), jnp.float32, low / len(cuts), top_value / len(cuts))
        return jnp.repeat(jnp.exp(heights), dims[axis_at] // parts).reshape((-1,) + (1,) * (len(dims) - axis_at - 1))

    factor_of = one(*cuts[0])
    for cut in cuts[1:]:
        factor_of = factor_of * one(*cut)
    return factor_of


def assign_block(stream_key, own, number, rows, count, top, limit, lean):
    ranking = jax.random.permutation(stream_key, count)
    crowded, ordinary = load_shares(count, rows * top, limit, lean, True), load_shares(count, rows * top, limit, lean, False)
    places = jnp.arange(count)

    def named(tallies, offset_by):
        used = int((tallies > 0).sum())
        fixed = max(1, used // 4)
        moved = fixed + (places - fixed + offset_by * (used - fixed)) % max(1, count - fixed)
        return jnp.zeros((count,), jnp.int32).at[ranking[jnp.where(places < fixed, places, moved)]].set(jnp.asarray(tallies, jnp.int32))

    tallies = jnp.where(number % 4 == 0, named(crowded, number // 4), named(ordinary, number - number // 4 - 1))
    mixed = jax.random.permutation(jax.random.fold_in(own, 3), count)
    donor, receiver = mixed[0:count // 2 * 2:2], mixed[1:count // 2 * 2:2]
    room = jnp.minimum(tallies[donor] - 1, limit - tallies[receiver]) // 2
    room = jnp.where((donor == ranking[0]) | (receiver == ranking[0]) | (tallies[receiver] == 0), 0, jnp.maximum(room, 0))
    moved = jax.random.randint(jax.random.fold_in(own, 4), (count // 2,), 0, 1 << 20) % (room + 1)
    tallies = tallies.at[donor].add(-moved).at[receiver].add(moved)
    labels = jnp.searchsorted(jnp.cumsum(tallies), jnp.arange(rows * top), side="right").astype(jnp.int32)
    table = labels.reshape(top, rows).T
    table = table[jax.random.permutation(jax.random.fold_in(own, 1), rows)]
    offset_by = jax.random.randint(jax.random.fold_in(own, 2), (rows, 1), 0, top)
    return jnp.take_along_axis(table, (jnp.arange(top)[None, :] + offset_by) % top, axis=1)


def load_shares(count, total, bound, slope, full):
    portions = [(1 << 20) // math.isqrt(rank ** slope) + 1 for rank in range(1, count + 1)]
    largest = bound if full else min(bound, max(-(-total // count), total * portions[0] // sum(portions)))
    least = 1 if total - largest >= count - 1 else 0
    given, surplus = [largest] + [least] * (count - 1), total - largest - least * (count - 1)
    while surplus > 0:
        free = [i for i in range(1, count) if given[i] < largest] or [i for i in range(1, count) if given[i] < bound]
        pool, left = sum([portions[i] for i in free]), surplus
        for i in free:
            more = min(bound - given[i], max(1, left * portions[i] // pool), surplus)
            given[i] = given[i] + more
            surplus = surplus - more
    return np.array(given)


def noise(key, extent, scale, reach, cuts=(), kind=jnp.bfloat16):
    loudness = levels(key, extent, cuts, -0.22, 0.18) if cuts else 1.0
    array = jax.random.normal(key, extent, jnp.float32) * scale * loudness
    return jnp.minimum(jnp.maximum(array, -reach), reach).astype(kind)


def setup_inputs(seed: int = 0) -> dict:
    key_of = jax.random.split(jax.random.key(seed), 7)
    blocks = noise(key_of[0], (BLOCKS, ROWS, NB), 0.0625, 0.375, ((0, 256),))
    counts = touch_ends(jax.random.randint(key_of[1], (BLOCKS,), 1, ROWS + 1), jax.random.fold_in(key_of[1], 1), 1, ROWS).astype(jnp.int32)
    owner_keys = jax.random.split(jax.random.fold_in(key_of[2], 1), BLOCKS // BLK_DEV)
    owner_turns = jax.random.permutation(jax.random.fold_in(key_of[2], 3), BLOCKS // BLK_DEV)
    owner = jax.vmap(lambda own, number: assign_block(jax.random.fold_in(key_of[2], 2), own, number, BLK_DEV, N_GY * N_GZ, 1, 1, 2))(owner_keys, owner_turns).reshape((BLOCKS, 1))
    kdiag = jnp.clip(jnp.exp(math.log(4.0) - 2.0794415 * jax.random.uniform(key_of[3], (SUBDOMAINS, NB), jnp.float32) ** levels(key_of[3], (SUBDOMAINS, NB), ((0, 256),), -0.2, 0.2)), 0.5, 4.0)
    rhs = draw_rhs(jax.random.fold_in(key_of[6], 71), 0)
    modes = noise(key_of[5], (SUBDOMAINS, NC, NB), 1.0, 6.0, ((0, 256),), jnp.float32)
    return dict(blocks=blocks, counts=counts, owner=owner, kdiag=kdiag, rhs=rhs, modes=modes)


def assemble(values):
    count = values.shape[1]
    width = values.shape[2]
    face = width // 8
    grid = values.reshape(N_GX, N_GY, N_GZ, count, width)
    next_x = jnp.roll(grid, -1, axis=0)
    prev_x = jnp.roll(grid, 1, axis=0)
    next_y = jnp.roll(grid, -1, axis=1)
    prev_y = jnp.roll(grid, 1, axis=1)
    next_z = jnp.roll(grid, -1, axis=2)
    prev_z = jnp.roll(grid, 1, axis=2)
    extra = jnp.concatenate([next_x[..., face:2 * face], prev_x[..., 0:face], next_y[..., 3 * face:4 * face], prev_y[..., 2 * face:3 * face], next_z[..., 6 * face:8 * face], prev_z[..., 4 * face:6 * face]], axis=-1)
    return (grid + extra).reshape(values.shape)

def reference(blocks, counts, owner, kdiag, rhs, modes):
    hi = lax.Precision.HIGHEST
    rowid = jnp.arange(ROWS, dtype=jnp.int32)[None, :, None]
    live = jnp.where(rowid < counts[:, None, None], blocks, jnp.zeros_like(blocks)).astype(jnp.float32)
    group = N_GY * N_GZ
    reader = jnp.arange(BLOCKS, dtype=jnp.int32) // BLK_DEV
    target = (reader // group * group + owner[:, 0]).astype(jnp.int32)
    start = jnp.eye(NB, dtype=jnp.float32)[None, :, :] * kdiag[:, :, None]

    def add_block(total, item):
        piece, where = item
        gram = jnp.dot(piece.T, piece, precision=hi)
        return (total.at[where].add(gram), None)
    stiff, _ = lax.scan(add_block, start, (live, target))
    schur = stiff.astype(jnp.bfloat16)
    loaded = assemble(jnp.concatenate([rhs[:, None, :], modes], axis=1))
    force = loaded[:, 0]
    basis = loaded[:, 1:]
    coarse = 0.5 * jnp.einsum('dcn,den->ce', basis, basis, precision=hi)
    gforce = 0.5 * jnp.einsum('dcn,dn->c', basis, force, precision=hi)
    fnorm = 0.5 * jnp.sum(force * force)
    factor = jnp.linalg.cholesky(coarse)
    coef = jax.scipy.linalg.cho_solve((factor, True), gforce)
    residual = force - jnp.einsum('c,dcn->dn', coef, basis, precision=hi)
    norm_now = fnorm - jnp.dot(gforce, coef, precision=hi)
    direction = residual
    solution = jnp.zeros_like(force)
    for step in range(ITERS):
        local = jnp.einsum('dij,dj->di', stiff, direction, precision=hi)
        image = assemble(local[:, None, :])[:, 0]
        gimage = 0.5 * jnp.einsum('dcn,dn->c', basis, image, precision=hi)
        coef = jax.scipy.linalg.cho_solve((factor, True), gimage)
        along = image - jnp.einsum('c,dcn->dn', coef, basis, precision=hi)
        alpha = norm_now / (0.5 * jnp.sum(direction * along))
        solution = solution + alpha * direction
        residual = residual - alpha * along
        norm_next = 0.5 * jnp.sum(residual * residual)
        direction = residual + norm_next / norm_now * direction
        norm_now = norm_next
    return (schur, solution, residual)
```

```python
import functools

import jax
import jax.numpy as jnp
from jax import lax
from jax.experimental import pallas as pl
from jax.experimental.pallas import tpu as pltpu
from jax.sharding import Mesh
from jax.sharding import PartitionSpec as P

GX_GY_GZ = ("gx_0", "gx_1", "gy", "gz")
GX = ("gx_0", "gx_1")
HI = lax.Precision.HIGHEST
CUTS = (96, 32)
STEP = 4


def ring(axis, shift):
    n = lax.axis_size(axis)
    return [(i, (i + shift) % n) for i in range(n)]


def assembled(values):
    f = values.shape[1] // 8
    spans = ((0, f), (f, 2 * f), (2 * f, 3 * f), (3 * f, 4 * f), (4 * f, 6 * f), (6 * f, 8 * f))
    extra = []
    for axis, (plus, minus) in zip((GX, "gy", "gz"), (spans[0:2], spans[2:4], spans[4:6])):
        extra.append(lax.ppermute(values[:, minus[0] : minus[1]], axis, ring(axis, -1)))
        extra.append(lax.ppermute(values[:, plus[0] : plus[1]], axis, ring(axis, 1)))
    return values + jnp.concatenate(extra, axis=1)


def pack_body(cuts, slot, live, *refs):
    step = pl.program_id(0)
    ins, outs = refs[:STEP], refs[STEP:]
    nrows, width = ins[0].shape[1:]
    rows = lax.broadcasted_iota(jnp.int32, (nrows, width), 0)
    for k in range(STEP):
        x = ins[k][0]
        x = jnp.where(rows < live[step * STEP + k], x, jnp.zeros_like(x))
        start = 0
        for out, size in zip(outs, cuts):
            out[k] = x[start : start + size]
            start += size


def pack(blocks, counts, owner, owners):
    nblk, nrows, width = blocks.shape
    hit = owner[:, 0][None, :] == lax.broadcasted_iota(jnp.int32, (owners, nblk), 0)
    slot = jnp.sum(jnp.where(hit, jnp.arange(nblk, dtype=jnp.int32)[None, :], 0), axis=1)
    live = jnp.sum(jnp.where(hit, counts[None, :], 0), axis=1)

    def source(k):
        return lambda i, slot, live: (slot[i * STEP + k], 0, 0)

    return pl.pallas_call(
        functools.partial(pack_body, CUTS),
        grid_spec=pltpu.PrefetchScalarGridSpec(
            num_scalar_prefetch=2,
            grid=(owners // STEP,),
            in_specs=[pl.BlockSpec((1, nrows, width), source(k)) for k in range(STEP)],
            out_specs=[pl.BlockSpec((STEP, c, width), lambda i, *_: (i, 0, 0)) for c in CUTS],
        ),
        out_shape=[jax.ShapeDtypeStruct((owners, c, width), blocks.dtype) for c in CUTS],
        name="pack",
    )(slot, live, *([blocks] * STEP))


def everyone(tile, axes):
    n = 1
    for axis in axes:
        n *= lax.axis_size(axis)
    copies = jnp.broadcast_to(tile[None], (n, *tile.shape))
    return jnp.sum(lax.all_to_all(copies, axes, 0, 0, tiled=True), axis=0)


def coefficients(g, nv):
    row = lax.broadcasted_iota(jnp.int32, g.shape, 0)
    col = lax.broadcasted_iota(jnp.int32, g.shape, 1)
    e = g
    for j in range(1, nv):
        pivot = jnp.sum(jnp.where(row == j, e, 0.0), axis=0, keepdims=True)
        column = jnp.sum(jnp.where(col == j, e, 0.0), axis=1, keepdims=True)
        corner = jnp.sum(jnp.where(col[:1] == j, pivot, 0.0), axis=1, keepdims=True)
        scaled = pivot / corner
        e = jnp.where(row == j, scaled, jnp.where(row == 0, e, e - column * scaled))
    e = jnp.where(row == 0, 0.0, e)

    def part(a, k):
        return a[:, k * nv : (k + 1) * nv]

    r8 = lax.broadcasted_iota(jnp.int32, (g.shape[0], nv), 0)
    c8 = lax.broadcasted_iota(jnp.int32, (g.shape[0], nv), 1)

    def as_row(v):
        return jnp.sum(jnp.where(r8 == c8, v, 0.0), axis=0, keepdims=True)

    def times(a, v_row):
        return jnp.sum(a * v_row, axis=1, keepdims=True)

    def dot(u, v):
        return jnp.sum(u * v, axis=0, keepdims=True)

    ga, gb, gc, gd = (part(g, k) for k in range(4))
    ib, ic = part(e, 1), part(e, 2)
    c0 = e[:, 0:1]
    first = jnp.where(r8[:, :1] == 0, 1.0, 0.0)
    q = first - c0
    rr = ga[0:1, 0:1] - dot(ga[:, 0:1] * (1.0 - first), c0)
    qr = as_row(q)
    p1 = times(ib, qr)
    p1r = as_row(p1)
    gbq, gaq = times(gb, qr), times(ga, qr)
    curve = dot(q, gbq) - dot(p1, gaq)
    alpha = rr / curve
    a = q + alpha * p1
    b = -alpha * q
    ar, br = qr + alpha * p1r, -alpha * qr
    gcb = times(gc, br)
    rr1 = dot(a, times(ga, ar)) + 2.0 * dot(a, times(gb, br)) + dot(b, gcb)
    beta = rr1 / rr
    d = a + beta * q
    dr = ar + beta * qr
    p2 = times(ib, dr) + times(ic, br)
    curve2 = (
        dot(d, times(gb, dr))
        + 2.0 * dot(d, gcb)
        + dot(b, times(gd, br))
        - dot(p2, times(ga, dr))
        - dot(p2, times(gb, br))
    )
    alpha2 = rr1 / curve2
    sol = (alpha * q + alpha2 * d, alpha2 * b)
    res = (a + alpha2 * p2, b - alpha2 * d, -alpha2 * b)
    return sol, res


def finish_body(nv, parts_ref, x_ref, w_ref, z_ref, sol_ref, res_ref):
    g = parts_ref[0]
    for i in range(1, parts_ref.shape[0]):
        g = g + parts_ref[i]
    sol, res = coefficients(g, nv)
    x, w, z = x_ref[...], w_ref[...], z_ref[...]
    sol_ref[...] = jnp.sum(sol[0][:nv] * x + sol[1][:nv] * w, axis=0, keepdims=True)
    res_ref[...] = jnp.sum(res[0][:nv] * x + res[1][:nv] * w + res[2][:nv] * z, axis=0, keepdims=True)


def shards(blocks, counts, owner, kdiag, rhs, modes):
    width = blocks.shape[2]
    owners = lax.axis_size("gy") * lax.axis_size("gz")
    x = assembled(jnp.concatenate([rhs, modes[0]], axis=0))
    nv = x.shape[0]
    stiff = jnp.diag(kdiag[0])
    for outgoing in pack(blocks, counts, owner, owners):
        arrived = lax.all_to_all(outgoing, ("gy", "gz"), split_axis=0, concat_axis=0, tiled=True)
        flat = arrived.reshape(-1, width)
        stiff = stiff + lax.dot_general(
            flat, flat, (((0,), (0,)), ((), ())), preferred_element_type=jnp.float32
        )
    schur = stiff.astype(jnp.bfloat16)[None]
    v1 = jnp.dot(x, stiff, precision=HI)
    w = assembled(v1)
    v2 = jnp.dot(w, stiff, precision=HI)
    near = jnp.dot(x, 0.5 * jnp.concatenate([x, w], axis=0).T, precision=HI)
    far = jnp.dot(w, jnp.concatenate([0.5 * w, v2], axis=0).T, precision=HI)
    mine = jnp.concatenate([near, far], axis=1)
    mine = jnp.pad(mine, ((0, 8 - nv), (0, 128 - 4 * nv)))
    z = assembled(v2)
    some = everyone(mine, ("gy", "gz"))
    gx = lax.axis_size(GX)
    parts = lax.all_to_all(jnp.broadcast_to(some[None], (gx, 8, 128)), GX, 0, 0, tiled=True)
    sol, res = pl.pallas_call(
        functools.partial(finish_body, nv),
        out_shape=[jax.ShapeDtypeStruct((1, width), jnp.float32)] * 2,
        name="finish",
    )(parts, x, w, z)
    return (schur, sol, res)


def solution(mesh):
    split = Mesh(mesh.devices.reshape(4, 2, mesh.shape["gy"], mesh.shape["gz"]), GX_GY_GZ)
    in_specs = (
        P(GX_GY_GZ, None, None),
        P(GX_GY_GZ),
        P(GX_GY_GZ, None),
        P(GX_GY_GZ, None),
        P(GX_GY_GZ, None),
        P(GX_GY_GZ, None, None),
    )
    out_specs = (P(GX_GY_GZ, None, None), P(GX_GY_GZ, None), P(GX_GY_GZ, None))
    return jax.shard_map(
        shards, mesh=split, in_specs=in_specs, out_specs=out_specs, check_vma=False
    )
```

```python
import functools

import jax
import jax.numpy as jnp
from jax import lax
from jax.experimental import pallas as pl
from jax.experimental.pallas import tpu as pltpu
from jax.sharding import Mesh
from jax.sharding import PartitionSpec as P

GX_GY_GZ = ("gx_0", "gx_1", "gy", "gz")
GX = ("gx_0", "gx_1")
HI = lax.Precision.HIGHEST
CUTS = (112, 16)
STEP = 4


def ring(axis, shift):
    n = lax.axis_size(axis)
    return [(i, (i + shift) % n) for i in range(n)]


def assembled(values):
    f = values.shape[1] // 8
    spans = ((0, f), (f, 2 * f), (2 * f, 3 * f), (3 * f, 4 * f), (4 * f, 6 * f), (6 * f, 8 * f))
    extra = []
    for axis, (plus, minus) in zip((GX, "gy", "gz"), (spans[0:2], spans[2:4], spans[4:6])):
        extra.append(lax.ppermute(values[:, minus[0] : minus[1]], axis, ring(axis, -1)))
        extra.append(lax.ppermute(values[:, plus[0] : plus[1]], axis, ring(axis, 1)))
    return values + jnp.concatenate(extra, axis=1)


def pack_body(cuts, slot, live, *refs):
    step = pl.program_id(0)
    ins, outs = refs[:STEP], refs[STEP:]
    nrows, width = ins[0].shape[1:]
    rows = lax.broadcasted_iota(jnp.int32, (nrows, 128), 0)
    for k in range(STEP):
        keep = rows < live[step * STEP + k]
        for c in range(0, width, 128):
            x = ins[k][0, :, c : c + 128]
            x = jnp.where(keep, x, jnp.zeros_like(x))
            start = 0
            for out, size in zip(outs, cuts):
                out[k, :, c : c + 128] = x[start : start + size]
                start += size


def pack(blocks, counts, owner, owners):
    nblk, nrows, width = blocks.shape
    hit = owner[:, 0][None, :] == lax.broadcasted_iota(jnp.int32, (owners, nblk), 0)
    slot = jnp.sum(jnp.where(hit, jnp.arange(nblk, dtype=jnp.int32)[None, :], 0), axis=1)
    live = jnp.sum(jnp.where(hit, counts[None, :], 0), axis=1)

    def source(k):
        return lambda i, slot, live: (slot[i * STEP + k], 0, 0)

    return pl.pallas_call(
        functools.partial(pack_body, CUTS),
        grid_spec=pltpu.PrefetchScalarGridSpec(
            num_scalar_prefetch=2,
            grid=(owners // STEP,),
            in_specs=[pl.BlockSpec((1, nrows, width), source(k)) for k in range(STEP)],
            out_specs=[pl.BlockSpec((STEP, c, width), lambda i, *_: (i, 0, 0)) for c in CUTS],
        ),
        out_shape=[jax.ShapeDtypeStruct((owners, c, width), blocks.dtype) for c in CUTS],
        name="pack",
    )(slot, live, *([blocks] * STEP))


def everyone(tile, axes):
    n = 1
    for axis in axes:
        n *= lax.axis_size(axis)
    copies = jnp.broadcast_to(tile[None], (n, *tile.shape))
    return jnp.sum(lax.all_to_all(copies, axes, 0, 0, tiled=True), axis=0)


def coefficients(g, nv):
    row = lax.broadcasted_iota(jnp.int32, g.shape, 0)
    col = lax.broadcasted_iota(jnp.int32, g.shape, 1)
    e = g
    for j in range(1, nv):
        pivot = jnp.sum(jnp.where(row == j, e, 0.0), axis=0, keepdims=True)
        column = jnp.sum(jnp.where(col == j, e, 0.0), axis=1, keepdims=True)
        corner = jnp.sum(jnp.where(col[:1] == j, pivot, 0.0), axis=1, keepdims=True)
        scaled = pivot / corner
        e = jnp.where(row == j, scaled, jnp.where(row == 0, e, e - column * scaled))
    e = jnp.where(row == 0, 0.0, e)

    def part(a, k):
        return a[:, k * nv : (k + 1) * nv]

    r8 = lax.broadcasted_iota(jnp.int32, (g.shape[0], nv), 0)
    c8 = lax.broadcasted_iota(jnp.int32, (g.shape[0], nv), 1)

    def as_row(v):
        return jnp.sum(jnp.where(r8 == c8, v, 0.0), axis=0, keepdims=True)

    def times(a, v_row):
        return jnp.sum(a * v_row, axis=1, keepdims=True)

    def dot(u, v):
        return jnp.sum(u * v, axis=0, keepdims=True)

    ga, gb, gc, gd = (part(g, k) for k in range(4))
    ib, ic = part(e, 1), part(e, 2)
    c0 = e[:, 0:1]
    first = jnp.where(r8[:, :1] == 0, 1.0, 0.0)
    q = first - c0
    rr = ga[0:1, 0:1] - dot(ga[:, 0:1] * (1.0 - first), c0)
    qr = as_row(q)
    p1 = times(ib, qr)
    p1r = as_row(p1)
    gbq, gaq = times(gb, qr), times(ga, qr)
    curve = dot(q, gbq) - dot(p1, gaq)
    alpha = rr / curve
    a = q + alpha * p1
    b = -alpha * q
    ar, br = qr + alpha * p1r, -alpha * qr
    gcb = times(gc, br)
    rr1 = dot(a, times(ga, ar)) + 2.0 * dot(a, times(gb, br)) + dot(b, gcb)
    beta = rr1 / rr
    d = a + beta * q
    dr = ar + beta * qr
    p2 = times(ib, dr) + times(ic, br)
    curve2 = (
        dot(d, times(gb, dr))
        + 2.0 * dot(d, gcb)
        + dot(b, times(gd, br))
        - dot(p2, times(ga, dr))
        - dot(p2, times(gb, br))
    )
    alpha2 = rr1 / curve2
    sol = (alpha * q + alpha2 * d, alpha2 * b)
    res = (a + alpha2 * p2, b - alpha2 * d, -alpha2 * b)
    return sol, res


def finish_body(nv, parts_ref, x_ref, w_ref, z_ref, sol_ref, res_ref):
    g = parts_ref[0]
    for i in range(1, parts_ref.shape[0]):
        g = g + parts_ref[i]
    sol, res = coefficients(g, nv)
    x, w, z = x_ref[...], w_ref[...], z_ref[...]
    sol_ref[...] = jnp.sum(sol[0][:nv] * x + sol[1][:nv] * w, axis=0, keepdims=True)
    res_ref[...] = jnp.sum(res[0][:nv] * x + res[1][:nv] * w + res[2][:nv] * z, axis=0, keepdims=True)


def shards(blocks, counts, owner, kdiag, rhs, modes):
    width = blocks.shape[2]
    owners = lax.axis_size("gy") * lax.axis_size("gz")
    chunks = [
        lax.all_to_all(outgoing, ("gy", "gz"), split_axis=0, concat_axis=0, tiled=True)
        for outgoing in pack(blocks, counts, owner, owners)
    ]
    stiff = jnp.diag(kdiag[0])
    for arrived in chunks[:-1]:
        flat = arrived.reshape(-1, width)
        stiff = stiff + lax.dot_general(
            flat, flat, (((0,), (0,)), ((), ())), preferred_element_type=jnp.float32
        )
    x = jnp.concatenate([rhs, modes[0]], axis=0)
    x, stiff = lax.optimization_barrier((x, stiff))
    x = assembled(x)
    nv = x.shape[0]
    flat = chunks[-1].reshape(-1, width)
    stiff = stiff + lax.dot_general(
        flat, flat, (((0,), (0,)), ((), ())), preferred_element_type=jnp.float32
    )
    v1 = jnp.dot(x, stiff, precision=HI)
    w = assembled(v1)
    v2 = jnp.dot(w, stiff, precision=HI)
    near = jnp.dot(x, 0.5 * jnp.concatenate([x, w], axis=0).T, precision=HI)
    far = jnp.dot(w, jnp.concatenate([0.5 * w, v2], axis=0).T, precision=HI)
    mine = jnp.concatenate([near, far], axis=1)
    mine = jnp.pad(mine, ((0, 8 - nv), (0, 128 - 4 * nv)))
    z = assembled(v2)
    some = everyone(mine, ("gy", "gz"))
    some, late = lax.optimization_barrier((some, stiff))
    schur = late.astype(jnp.bfloat16)[None]
    gx = lax.axis_size(GX)
    parts = lax.all_to_all(jnp.broadcast_to(some[None], (gx, 8, 128)), GX, 0, 0, tiled=True)
    sol, res = pl.pallas_call(
        functools.partial(finish_body, nv),
        out_shape=[jax.ShapeDtypeStruct((1, width), jnp.float32)] * 2,
        name="finish",
    )(parts, x, w, z)
    return (schur, sol, res)


def solution(mesh):
    split = Mesh(mesh.devices.reshape(4, 2, mesh.shape["gy"], mesh.shape["gz"]), GX_GY_GZ)
    in_specs = (
        P(GX_GY_GZ, None, None),
        P(GX_GY_GZ),
        P(GX_GY_GZ, None),
        P(GX_GY_GZ, None),
        P(GX_GY_GZ, None),
        P(GX_GY_GZ, None, None),
    )
    out_specs = (P(GX_GY_GZ, None, None), P(GX_GY_GZ, None), P(GX_GY_GZ, None))
    return jax.shard_map(
        shards, mesh=split, in_specs=in_specs, out_specs=out_specs, check_vma=False
    )
```
